128 devices in a mesh: seq: 32 (over y, x_hi, z), wt: 4 (over x_lo, core).
Axes of the slice: x: 4 (x_hi: 2, x_lo: 2; x = x_hi * 2 + x_lo), y: 4, z: 4, core: 2. Of those that a mesh axis runs over, the one named last changes fastest.
Arguments:
- activations: bfloat16 [65536, 1536], P('seq', 'wt'), may hold values from -6 to 6
- first_norm_scale: float32 [1536], P('wt'), may hold values from 0.1 to 1.9
- first_norm_shift: float32 [1536], P('wt'), may hold values from -0.5 to 0.5
- first_kernel_weight: bfloat16 [3, 1536, 1536], P(None, 'seq', 'wt'), may hold values from -0.09375 to 0.09375
- second_norm_scale: float32 [1536], P('wt'), may hold values from 0.1 to 1.9
- second_norm_shift: float32 [1536], P('wt'), may hold values from -0.5 to 0.5
- second_kernel_weight: bfloat16 [3, 1536, 1536], P(None, 'seq', 'wt'), may hold values from -0.09375 to 0.09375
Outputs:
- tower_out: bfloat16 [65536, 1536], P('seq', 'wt')
The draws below stay inside these ranges and needn't reach their ends.
All inputs are finite; a program needn't handle non-finite values.
Results may differ from the reference program's by a relative error of at most 0.008.
Values may be sent and summed in bfloat16 or wider, within the bound.
No kernel may reach another device: no remote copies, remote signals or barrier semaphores. Data moves between devices by JAX's collectives and lax.ppermute only.
A program may use at most 64 MiB of HBM per device.

```python
import jax
import jax.numpy as jnp

C = 1536
DILATION_FIRST = 256
DILATION_SECOND = 512
LENGTH = 65536


def block_scale(rng, extent, pieces, smallest, largest):
    gain = 1.0
    for dim, parts in pieces:
        steps = jax.random.uniform(jax.random.fold_in(jax.random.fold_in(rng, 6), dim), (parts,), jnp.float32, smallest / len(pieces), largest / len(pieces))
        gain = gain * jnp.repeat(jnp.exp(steps), extent[dim] // parts).reshape((-1,) + (1,) * (len(extent) - 1 - dim))
    return gain


def scatter_about(key, dims, deviation, limit, cuts=(), dtype=jnp.bfloat16):
    gain = block_scale(key, dims, cuts, -0.22, 0.18) if cuts else 1.0
    entries = jax.random.normal(key, dims, jnp.float32) * deviation * gain
    return jnp.minimum(jnp.maximum(entries, -limit), limit).astype(dtype)


def setup_inputs(seed: int = 0) -> dict:
    keys = jax.random.split(jax.random.key(seed), 8)
    return {
        "activations": scatter_about(keys[0], (LENGTH, C), 1.0, 6.0, ((0, 32), (1, 4))),
        "first_norm_scale": jnp.clip(1.0 + 0.18 * jax.random.normal(keys[1], (C,), jnp.float32), 0.1, 1.9),
        "first_norm_shift": jnp.clip(jax.random.uniform(keys[2], (C,), jnp.float32, -0.5, 0.5) * block_scale(keys[2], (C,), ((0, 4),), -0.4, 0.0), -0.5, 0.5),
        "first_kernel_weight": scatter_about(keys[3], (3, C, C), (3 * C) ** -0.5, 0.09375, ((1, 32), (2, 4))),
        "second_norm_scale": jnp.clip(1.0 + 0.18 * jax.random.normal(keys[4], (C,), jnp.float32), 0.1, 1.9),
        "second_norm_shift": jnp.clip(jax.random.uniform(keys[5], (C,), jnp.float32, -0.5, 0.5) * block_scale(keys[5], (C,), ((0, 4),), -0.4, 0.0), -0.5, 0.5),
        "second_kernel_weight": scatter_about(keys[6], (3, C, C), (3 * C) ** -0.5, 0.09375, ((1, 32), (2, 4))),
    }


def single_conv_layer(state, scale, shift, weight, reach):
    value = state.astype(jnp.float32) * scale[None, :] + shift[None, :]
    hidden = jax.nn.gelu(value, approximate=True).astype(jnp.bfloat16)
    total_rows = hidden.shape[0]
    padded = jnp.pad(hidden, ((reach, reach), (0, 0)))
    total = jnp.zeros((total_rows, hidden.shape[1]), jnp.float32)
    for tap in range(3):
        total = total + jnp.dot(padded[tap * reach:tap * reach + total_rows], weight[tap], preferred_element_type=jnp.float32)
    return (state.astype(jnp.float32) + total).astype(jnp.bfloat16)


def reference(activations, first_norm_scale, first_norm_shift, first_kernel_weight, second_norm_scale, second_norm_shift, second_kernel_weight):
    first_conv_layer = single_conv_layer(activations, first_norm_scale, first_norm_shift, first_kernel_weight, DILATION_FIRST)
    return single_conv_layer(first_conv_layer, second_norm_scale, second_norm_shift, second_kernel_weight, DILATION_SECOND)
```

```python
import functools

import jax
import jax.numpy as jnp
from jax import lax
from jax.experimental import pallas as pl
from jax.experimental.pallas import tpu as pltpu
from jax.sharding import PartitionSpec as P


AXES = ("seq", "wt")
HALF = 768
WIDE = 1536
ROWS = 128
REL = (0, -1, 1, 2)


def linear(y, x, z, c):
    return ((y * 2 + x // 2) * 4 + z) * 4 + (x % 2) * 2 + c


def pairs(move):
    out = []
    for y in range(4):
        for x in range(4):
            for z in range(4):
                for c in range(2):
                    to = move(y, x, z, c)
                    if to is not None:
                        ty, tx, tz, tc = to
                        out.append((linear(y, x, z, c), linear(ty % 4, tx % 4, tz % 4, tc)))
    return out


def following(y, x, z, c):
    if z < 3:
        return y, x, z + 1, c
    if x < 2:
        return y, 3 - x, 0, c
    return (y + 1, 3 - x, 0, c) if y < 3 else None


SIBLING = pairs(lambda y, x, z, c: (y, x, z, 1 - c))
ACROSS = pairs(lambda y, x, z, c: (y, x ^ 1, z, c))
NEXT = pairs(following)
PREVIOUS = [(b, a) for a, b in NEXT]
OPEN_ONE = pairs(lambda y, x, z, c: (y, x ^ 2, z, 1) if c == 0 else (y, x, z, 0))
OPEN_TWO = pairs(lambda y, x, z, c: (y, x ^ 2, z, 1) if c == 1 else None)


def ring_one(step):
    return pairs(lambda y, x, z, c: (y, x, z + step, c) if c == 0 else (y + step, x, z, c))


def ring_two(step):
    return pairs(lambda y, x, z, c: (y + step, x, z, c) if c == 0 else (y, x, z + step, c))


def send(cells, route):
    return lax.ppermute(cells, AXES, route)


def gelu(value):
    return jax.nn.gelu(value, approximate=True)


def gathered(weights, core):
    own = jnp.stack(weights)
    first = send(own, OPEN_ONE)
    second = send(own, OPEN_TWO)
    block = jnp.concatenate(
        [jnp.where(core == 0, own, first), jnp.where(core == 0, first, second)], axis=-1
    )
    parts = [block] + [send(block, ring_one(step)) for step in (1, -1, 2)]
    out = []
    for layer in range(2):
        whole = jnp.stack([part[layer] for part in parts])
        up = send(whole, ring_two(1))
        down = send(whole, ring_two(-1))
        far_up = send(up[:2], ring_two(1))
        far_down = send(down[2:], ring_two(-1))
        mine = (whole, up, down, far_up, far_down)
        out.append(mine + tuple(send(part, SIBLING) for part in mine))
    return out


def weight_copies(parts, landed, sems, tile):
    seq = lax.axis_index("seq")
    wt = lax.axis_index("wt")
    z, x_hi, y = lax.rem(seq, 4), lax.rem(lax.div(seq, 4), 2), lax.div(seq, 8)
    x_lo, core = lax.div(wt, 2), lax.rem(wt, 2)
    copies = []
    layout = ((0, range(4)), (-1, range(4)), (1, range(4)), (2, range(2)), (2, range(2, 4)))
    for owner in range(2):
        color = core if owner == 0 else 1 - core
        xb = jnp.where(color == 0, x_hi, 1 - x_hi)
        for part, (far, span) in enumerate(layout):
            ref = parts[owner * 5 + part]
            for slot, index in enumerate(span):
                near = REL[index]
                zb = lax.rem(z + 4 + jnp.where(color == 0, near, far), 4)
                yb = lax.rem(y + 4 + jnp.where(color == 0, far, near), 4)
                half = lax.rem(lax.div(yb, 2) + x_lo, 2)
                row = half * HALF + lax.rem(yb, 2) * 384 + (xb * 4 + zb) * 48
                columns = pl.ds(tile * 256, 256)
                copies.append(
                    pltpu.make_async_copy(
                        ref.at[slot, :, :, columns],
                        landed.at[:, pl.ds(pl.multiple_of(row, 48), 48), columns],
                        sems.at[tile],
                    )
                )
    return copies


def conv_kernel(plan, *refs):
    n_pieces = len(plan["pieces"])
    pieces, refs = refs[:n_pieces], refs[n_pieces:]
    parts, refs = refs[:10], refs[10:]
    n_states = len(plan["states"])
    states, refs = refs[:n_states], refs[n_states:]
    if plan["last"]:
        (out, hidden, weight, hidden_sem, weight_sems) = refs
    else:
        scale, shift, out, out_hidden, hidden, weight, hidden_sem, weight_sems = refs
    seq = lax.axis_index("seq")
    z = lax.rem(seq, 4)
    copies = []
    for ref, moves in zip(pieces, plan["pieces"]):
        for index, row, side in moves:
            count = plan["halo"] if side in ("left", "right") else ROWS
            if side == "left":
                turned = jnp.where(z == 0, 1, 0)
            elif side == "right":
                turned = jnp.where(z == 3, 1, 0)
            if side in ("left", "right"):
                column = pl.multiple_of(lax.rem(turned + index, 2) * HALF, HALF)
            else:
                column = side * HALF
            copies.append(
                pltpu.make_async_copy(
                    ref.at[index],
                    hidden.at[pl.ds(row * ROWS, count), pl.ds(column, HALF)],
                    hidden_sem,
                )
            )
    tiles = [weight_copies(parts, weight, weight_sems, tile) for tile in range(3)]
    for copy in copies:
        copy.start()
    for tile in tiles:
        for copy in tile:
            copy.start()
    for copy in copies:
        copy.wait()
    for tile in range(3):
        for copy in tiles[tile]:
            copy.wait()
        columns = pl.ds(tile * 256, 256)
        for start, place, source, source_row in plan["segments"]:
            total = None
            for tap in range(3):
                product = jnp.dot(
                    hidden[pl.ds(start + tap * plan["shift"], 256), :],
                    weight[tap, :, columns],
                    preferred_element_type=jnp.float32,
                )
                total = product if total is None else total + product
            state = states[source][pl.ds(source_row, 256), columns]
            layer = (state.astype(jnp.float32) + total).astype(jnp.bfloat16)
            out[pl.ds(place, 256), columns] = layer
            if not plan["last"]:
                value = layer.astype(jnp.float32) * scale[:, columns] + shift[:, columns]
                out_hidden[pl.ds(place, 256), columns] = gelu(value).astype(jnp.bfloat16)


def conv(plan, pieces, parts, states, norm):
    rows = sum(256 for _ in plan["segments"])
    shape = jax.ShapeDtypeStruct((rows, HALF), jnp.bfloat16)
    inputs = list(pieces) + list(parts) + list(states) + list(norm)
    anywhere = pl.BlockSpec(memory_space=pl.ANY)
    near = pl.BlockSpec(memory_space=pltpu.VMEM)
    outs = [shape] if plan["last"] else [shape, shape]
    return pl.pallas_call(
        functools.partial(conv_kernel, plan),
        out_shape=outs,
        in_specs=[anywhere] * (len(pieces) + len(parts)) + [near] * (len(states) + len(norm)),
        out_specs=[near] * len(outs),
        scratch_shapes=[
            pltpu.VMEM((plan["height"] * ROWS, WIDE), jnp.bfloat16),
            pltpu.VMEM((3, WIDE, HALF), jnp.bfloat16),
            pltpu.SemaphoreType.DMA(()),
            pltpu.SemaphoreType.DMA((3,)),
        ],
        compiler_params=pltpu.CompilerParams(vmem_limit_bytes=40 << 20),
        cost_estimate=pl.CostEstimate(
            flops=2 * rows * 3 * WIDE * HALF, bytes_accessed=8 << 20, transcendentals=0
        ),
        name=plan["name"],
    )(*inputs)


EDGE = {
    "name": "conv_edge",
    "height": 8,
    "halo": ROWS,
    "shift": ROWS,
    "last": False,
    "pieces": (
        ((0, 1, 0), (1, 6, 0)),
        ((0, 1, 1), (1, 6, 1)),
        ((0, 2, 0), (1, 3, 0), (2, 4, 0), (3, 5, 0)),
        ((0, 2, 1), (1, 3, 1), (2, 4, 1), (3, 5, 1)),
        ((0, 0, "left"), (1, 0, "left")),
        ((0, 7, "right"), (1, 7, "right")),
    ),
    "states": (0, 1),
    "segments": ((0, 0, 0, 0), (512, 256, 0, 1536 // 2)),
}


def plan_edge():
    plan = dict(EDGE)
    plan["states"] = (0,)
    plan["segments"] = ((0, 0, 0, 0), (512, 256, 0, 768))
    return plan


def plan_middle():
    return {
        "name": "conv_middle",
        "height": 6,
        "halo": ROWS,
        "shift": ROWS,
        "last": False,
        "pieces": (
            ((0, 0, 0), (1, 1, 0), (2, 4, 0), (3, 5, 0)),
            ((0, 0, 1), (1, 1, 1), (2, 4, 1), (3, 5, 1)),
            ((0, 2, 0), (1, 3, 0)),
            ((0, 2, 1), (1, 3, 1)),
        ),
        "states": (0,),
        "segments": ((0, 0, 0, 256), (256, 256, 0, 512)),
    }


def plan_last():
    return {
        "name": "conv_last",
        "height": 12,
        "halo": 2 * ROWS,
        "shift": 2 * ROWS,
        "last": True,
        "pieces": (
            ((0, 2, 0), (1, 3, 0), (2, 8, 0), (3, 9, 0)),
            ((0, 2, 1), (1, 3, 1), (2, 8, 1), (3, 9, 1)),
            ((0, 4, 0), (1, 5, 0), (2, 6, 0), (3, 7, 0)),
            ((0, 4, 1), (1, 5, 1), (2, 6, 1), (3, 7, 1)),
            ((0, 0, "left"), (1, 0, "left")),
            ((0, 10, "right"), (1, 10, "right")),
        ),
        "states": (0, 1),
        "segments": ((0, 0, 0, 0), (256, 256, 1, 0), (512, 512, 1, 256), (768, 768, 0, 256)),
    }


def shards(act, scale_one, shift_one, weight_one, scale_two, shift_two, weight_two):
    core = lax.rem(lax.axis_index("wt"), 2)
    layers = gathered((weight_one, weight_two), core)

    def joined(mine, other):
        return jnp.where(
            core == 0,
            jnp.concatenate([mine, other], axis=-1),
            jnp.concatenate([other, mine], axis=-1),
        )

    view = act.reshape(8, 2, ROWS, 384)
    keep = lax.dynamic_index_in_dim(view, core, 1, keepdims=False)
    give = lax.dynamic_index_in_dim(view, 1 - core, 1, keepdims=False)
    norm = jnp.stack([scale_one, shift_one, scale_two, shift_two])
    norms = joined(norm, send(norm, SIBLING))
    state = joined(keep, send(give, SIBLING))

    value = state.astype(jnp.float32) * norms[0] + norms[1]
    hidden = gelu(value).astype(jnp.bfloat16)
    edge = jnp.stack([hidden[0], hidden[7]])
    middle = jnp.concatenate([hidden[1:3], hidden[5:7]])
    inner = hidden[3:5]
    edge_far = send(edge, ACROSS)
    middle_far = send(middle, ACROSS)
    inner_far = send(inner, ACROSS)
    left = send(jnp.stack([edge[1], edge_far[1]]), NEXT)
    right = send(jnp.stack([edge[0], edge_far[0]]), PREVIOUS)

    flat = state.reshape(8 * ROWS, HALF)
    norm_two = (norms[2:3], norms[3:4])
    outer_one, outer_hidden = conv(
        plan_edge(), (edge, edge_far, middle, middle_far, left, right), layers[0], (flat,), norm_two
    )
    outer = outer_hidden.reshape(4, ROWS, HALF)
    outer_far = send(outer, ACROSS)
    inner_one, inner_hidden = conv(
        plan_middle(), (middle, middle_far, inner, inner_far), layers[0], (flat,), norm_two
    )
    core_two = inner_hidden.reshape(4, ROWS, HALF)
    core_far = send(core_two, ACROSS)

    def halo(part):
        return jnp.stack([part[0], part[1]]).reshape(2, 2 * ROWS, HALF)

    left = send(halo((outer[2:], outer_far[2:])), NEXT)
    right = send(halo((outer[:2], outer_far[:2])), PREVIOUS)
    (result,) = conv(
        plan_last(),
        (outer, outer_far, core_two, core_far, left, right),
        layers[1],
        (outer_one, inner_one),
        (),
    )
    result = result.reshape(8, ROWS, 2, 384)
    mine = lax.dynamic_index_in_dim(result, core, 2, keepdims=False)
    theirs = send(lax.dynamic_index_in_dim(result, 1 - core, 2, keepdims=False), SIBLING)
    whole = jnp.where(core == 0, jnp.stack([mine, theirs], 1), jnp.stack([theirs, mine], 1))
    return whole.reshape(2048, 384)


def solution(mesh):
    placed = (
        P("seq", "wt"),
        P("wt"),
        P("wt"),
        P(None, "seq", "wt"),
        P("wt"),
        P("wt"),
        P(None, "seq", "wt"),
    )
    return jax.shard_map(
        shards, mesh=mesh, in_specs=placed, out_specs=P("seq", "wt"), check_vma=False
    )
```
